32 devices in a mesh: groups: 2 (over x), ctx: 16 (over z, y, core).
Axes of the slice: x: 2, y: 2, z: 4, core: 2. Of those that a mesh axis runs over, the one named last changes fastest.
Arguments:
- queries: bfloat16 [2048, 256], P(('groups', 'ctx')), parts along dimension 0, may hold values from -60 to 60
- keys: bfloat16 [2048, 128], P(('groups', 'ctx')), parts along dimension 0, may hold values from -6 to 6
- values: bfloat16 [2048, 128], P(('groups', 'ctx')), parts along dimension 0, may hold values from -96 to 96
- span_section: int32 [32], P(('groups', 'ctx')), parts along dimension 0, may hold values from 0 to 7, as said below
- query_section: int32 [64], P('groups'), parts along dimension 0, may hold values from 0 to 7, as said below
- section_queries: bfloat16 [64, 256], P('groups'), parts along dimension 0, may hold values from -60 to 60
- out_proj: bfloat16 [256, 4608], replicated, may hold values from -0.375 to 0.375
- norm_gain: bfloat16 [4608], replicated, may hold values from 0.099609375 to 1.8984375
- up_weight: bfloat16 [4608, 4096], P(None, 'ctx'), may hold values from -0.09375 to 0.09375
- down_weight: bfloat16 [4096, 4608], P('ctx'), may hold values from -0.125 to 0.125
Outputs:
- context: bfloat16 [2048, 256], P(('groups', 'ctx')), parts along dimension 0
- section_out: bfloat16 [64, 4608], P('groups', 'ctx'), parts along dimension 0
The draws below stay inside these ranges and needn't reach their ends.
There are 2 independent parts, one for each index of `groups`. The reference program is written for one: setup_inputs(seed, part) draws one part's arguments, and reference() takes and returns one part's arrays. A program takes and returns all parts, laid end to end along the dimension named above; an argument that names none is the same for every part. Nothing has to cross between parts.
Inputs may be any that keep to these rules, and one draw needn't show every extreme that they name: `span_section`: sections are runs of whole spans in order; every section holds one span or more. `query_section`: every section is read by exactly 4 section queries.
All inputs are finite; a program needn't handle non-finite values.
Results may differ from the reference program's by a relative error of at most 0.018.
Values may be sent and summed in bfloat16 or wider, within the bound.
A program may use at most 128 MiB of HBM per device.

```python
import math
import jax
import jax.numpy as jnp
from jax import lax

D = 4608
HD = 128
HQ = 2
FF = 4096
SPAN = 64
TOKENS = 1024
NCHUNK = 16
SQ = 32
NSEC = 8


def section_plan(key):
    order = jax.random.permutation(jax.random.fold_in(key, 11), NCHUNK - 1)
    cuts = (jnp.sort(order[:NSEC - 1]) + 1).astype(jnp.int32)
    span_index = jnp.arange(NCHUNK, dtype=jnp.int32)
    span_ids = jnp.sum((cuts[None, :] <= span_index[:, None]).astype(jnp.int32), axis=1).astype(jnp.int32)
    reader = (jax.random.permutation(jax.random.fold_in(key, 12), SQ) % NSEC).astype(jnp.int32)
    return (span_ids, reader)


def float_plan(key):
    query_key = jax.random.fold_in(key, 21)
    key_key = jax.random.fold_in(key, 22)
    section_key = jax.random.fold_in(key, 23)
    base_q = 1.5 * jax.random.truncated_normal(query_key, -6.0, 6.0, (TOKENS, HQ * HD), jnp.float32)
    base_k = jax.random.truncated_normal(key_key, -6.0, 6.0, (TOKENS, HD), jnp.float32)
    base_s = 1.5 * jax.random.truncated_normal(section_key, -6.0, 6.0, (SQ, HQ * HD), jnp.float32)
    return (base_q, base_k, base_s)


def draw_queries(key, part):
    return float_plan(key)[0].astype(jnp.bfloat16)


def draw_keys(key, part):
    return float_plan(key)[1].astype(jnp.bfloat16)


def draw_section_queries(key, part):
    return float_plan(key)[2].astype(jnp.bfloat16)


def draw_span_section(key, part):
    return section_plan(key)[0]


def draw_query_section(key, part):
    return section_plan(key)[1]


def with_spikes(entries, rng, source, target, shards_of, factor):
    owner, partner = [(jnp.arange(entries.shape[position]) // (entries.shape[position] // shards_of)).reshape([-1 if axis == position else 1 for axis in range(entries.ndim)]) for position in (source, target)]
    chosen = jax.random.permutation(rng, shards_of)[partner]
    strong = (owner == chosen) | (owner == (partner + shards_of // 2) % shards_of)
    return jnp.where(strong, factor * entries, entries)


def block_levels(stream_key, extent, pieces, least, high):
    def one(axis_at, parts):
        steps = jax.random.uniform(jax.random.fold_in(jax.random.fold_in(stream_key, 6), axis_at), (parts,), jnp.float32, least / len(pieces), high / len(pieces))
        return jnp.repeat(jnp.exp(steps), extent[axis_at] // parts).reshape((-1,) + (1,) * (len(extent) - axis_at - 1))

    gain = one(*pieces[0])
    for cut in pieces[1:]:
        gain = gain * one(*cut)
    return gain


def centred(rng, extent, deviation, most, split=(), kind=jnp.bfloat16):
    level = block_levels(rng, extent, split, -0.22, 0.18) if split else 1.0
    entries = jax.random.normal(rng, extent, jnp.float32) * deviation * level
    return jnp.minimum(jnp.maximum(entries, -most), most).astype(kind)


def bell_draw_with(stream_key, shape, deviation, limit, cuts, heavy, held_as=jnp.bfloat16):
    array = deviation * jax.random.normal(stream_key, shape, jnp.float32)
    if cuts:
        array = array * block_levels(stream_key, shape, cuts, -0.22, 0.18)
    return jnp.clip(with_spikes(array, jax.random.fold_in(stream_key, 3), *heavy), -limit, limit).astype(held_as)


def setup_inputs(seed: int = 0, part: int = 0) -> dict:
    key_of = jax.random.split(jax.random.key(seed), 11)
    own_keys = jax.random.split(jax.random.fold_in(key_of[10], part), 11)
    queries = draw_queries(jax.random.fold_in(jax.random.fold_in(key_of[10], part), 71), part)
    keys = draw_keys(jax.random.fold_in(jax.random.fold_in(key_of[10], part), 71), part)
    values = centred(own_keys[2], (TOKENS, HD), 16.0, 96.0, ((0, 16),))
    span_section = draw_span_section(jax.random.fold_in(jax.random.fold_in(key_of[10], part), 71), part)
    query_section = draw_query_section(jax.random.fold_in(jax.random.fold_in(key_of[10], part), 71), part)
    section_queries = draw_section_queries(jax.random.fold_in(jax.random.fold_in(key_of[10], part), 71), part)
    out_proj = centred(key_of[6], (HQ * HD, D), (HQ * HD) ** -0.5, 0.375)
    norm_gain = jnp.clip(1.0 + 0.18 * jax.random.normal(key_of[7], (D,), jnp.float32), 0.099609375, 1.8984375).astype(jnp.bfloat16)
    up_weight = centred(key_of[8], (D, FF), D ** -0.5, 0.09375, ((1, 16),))
    down_weight = bell_draw_with(key_of[9], (FF, D), FF ** -0.5, 0.125, ((0, 16),), (0, 1, 16, 2.0))
    return {"queries": queries, "keys": keys, "values": values, "span_section": span_section, "query_section": query_section, "section_queries": section_queries, "out_proj": out_proj, "norm_gain": norm_gain, "up_weight": up_weight, "down_weight": down_weight}


def reference(queries, keys, values, span_section, query_section, section_queries, out_proj, norm_gain, up_weight, down_weight):
    scale = HD ** (-0.5)
    block_rows = math.gcd(256, TOKENS)

    def attend(query_block):
        count = query_block.shape[0]
        flat = query_block.reshape(count * HQ, HD)
        scores = jnp.dot(flat, keys.T, preferred_element_type=jnp.float32) * scale
        top = lax.optimization_barrier(jnp.max(scores, axis=1, keepdims=True))
        weights = jnp.exp(scores - top)
        total = lax.optimization_barrier(jnp.sum(weights, axis=1, keepdims=True))
        mixed = jnp.dot(weights.astype(jnp.bfloat16), values, preferred_element_type=jnp.float32) / total
        return mixed.reshape(count, HQ * HD).astype(jnp.bfloat16)
    context = lax.map(attend, queries.reshape(TOKENS // block_rows, block_rows, HQ * HD))
    context = context.reshape(TOKENS, HQ * HD)
    token_section = jnp.repeat(span_section, SPAN)
    admitted = (query_section[:, None] == token_section[None, :])[:, None, :]
    cross = jnp.dot(section_queries.reshape(SQ * HQ, HD), keys.T, preferred_element_type=jnp.float32) * scale
    cross = cross.reshape(SQ, HQ, TOKENS)
    top = lax.optimization_barrier(jnp.max(jnp.where(admitted, cross, jnp.float32(-1e+30)), axis=2, keepdims=True))
    cross_weights = jnp.where(admitted, jnp.exp(cross - top), jnp.float32(0.0))
    cross_total = lax.optimization_barrier(jnp.sum(cross_weights, axis=2))
    summed = jnp.einsum('shu,uhd->shd', cross_weights.astype(jnp.bfloat16).astype(jnp.float32), context.reshape(TOKENS, HQ, HD).astype(jnp.float32))
    pooled = (summed / cross_total[:, :, None]).reshape(SQ, HQ * HD).astype(jnp.bfloat16)
    embed = jnp.dot(pooled, out_proj, preferred_element_type=jnp.float32)
    normed = embed * lax.rsqrt(lax.optimization_barrier(jnp.mean(embed * embed, axis=1, keepdims=True)) + 1e-06) * norm_gain.astype(jnp.float32)
    normed = normed.astype(jnp.bfloat16)
    hidden = jax.nn.gelu(jnp.dot(normed, up_weight, preferred_element_type=jnp.float32)).astype(jnp.bfloat16)
    section_out = jnp.dot(hidden, down_weight, preferred_element_type=jnp.float32).astype(jnp.bfloat16)
    return (context, section_out)
```

```python
import functools

import jax
import jax.numpy as jnp
from jax import lax
from jax.experimental import pallas as pl
from jax.experimental.pallas import tpu as pltpu
from jax.sharding import PartitionSpec as P

HD = 128
HQ = 2
SPAN = 64
READERS = 4
CHUNK = 1024
SLOTS = HQ * READERS

F32 = jnp.float32
BF16 = jnp.bfloat16
MESH = pl.DeviceIdType.MESH


def each(low, high, body):
    if high - low <= 16:
        for k in range(low, high):
            body(k)
    else:
        pl.loop(low, high)(body)


def dims(a, b):
    return (((a,), (b,)), ((), ()))


def dot(a, b, ca=1, cb=0):
    return lax.dot_general(a, b, dims(ca, cb), preferred_element_type=F32)


def iota(shape, axis):
    return lax.broadcasted_iota(jnp.int32, shape, axis)


def kernel(
    n,
    q_ref,
    k_ref,
    v_ref,
    span_ref,
    qsec_ref,
    sq_ref,
    o_ref,
    gain_ref,
    up_ref,
    down_ref,
    ctx_ref,
    out_ref,
    kv,
    sec,
    part,
    gath,
    ov,
    upv,
    downv,
    yb,
    rb,
    sb,
    fb,
    wsem,
    kvsem,
    ag_send,
    ag_recv,
    rl_send,
    rl_recv,
    sc_send,
    sc_recv,
    pt_send,
    pt_recv,
    pr_send,
    pr_recv,
    fn_send,
    fn_recv,
):
    scale = HD ** (-0.5)
    chips = n // 2
    me = lax.axis_index("ctx")
    chip = me // 2
    core = me % 2
    partner = me + 1 - 2 * core
    rows = q_ref.shape[0]
    tokens = n * rows
    count = qsec_ref.shape[1]

    own = kv.at[me]
    kcopy = pltpu.make_async_copy(k_ref, own.at[:, 0:HD], kvsem.at[0])
    vcopy = pltpu.make_async_copy(v_ref, own.at[:, HD : 2 * HD], kvsem.at[1])
    kcopy.start()
    vcopy.start()
    weights = [
        pltpu.make_async_copy(o_ref, ov, wsem.at[0]),
        pltpu.make_async_copy(up_ref, upv, wsem.at[1]),
        pltpu.make_async_copy(down_ref, downv, wsem.at[2]),
    ]
    for w in weights:
        w.start()

    mine = jnp.broadcast_to(span_ref[0, 0], (1, HD))
    sec[me] = mine

    barrier = pltpu.get_barrier_semaphore()

    def greet(k):
        pl.semaphore_signal(
            barrier, inc=1, device_id={"ctx": lax.rem(me + k, n)}, device_id_type=MESH
        )

    each(1, n, greet)
    pl.semaphore_wait(barrier, n - 1)
    kcopy.wait()
    vcopy.wait()

    def remote(src, dst, send, recv, to):
        return pltpu.make_async_remote_copy(
            src_ref=src,
            dst_ref=dst,
            send_sem=send,
            recv_sem=recv,
            device_id={"ctx": to},
            device_id_type=MESH,
        )

    def gather_copy(k):
        to = lax.rem(chip + k, chips) * 2 + core
        return remote(own, own, ag_send.at[k - 1], ag_recv.at[k - 1], to)

    def arrived_block(k):
        return kv.at[lax.rem(chip - k + chips, chips) * 2 + core]

    def relay_copy(k):
        block = arrived_block(k)
        return remote(block, block, rl_send.at[k], rl_recv.at[k], partner)

    def section_copy(k):
        return remote(sec.at[me], sec.at[me], sc_send, sc_recv, lax.rem(me + k, n))

    each(1, chips, lambda k: gather_copy(k).start())
    relay_copy(0).start()
    each(1, n, lambda k: section_copy(k).start())

    qrow = jnp.broadcast_to(qsec_ref[...], (8, count)).astype(F32)
    eye = (iota((count, count), 0) == iota((count, count), 1)).astype(BF16)
    qcol = dot(eye, qrow.astype(BF16), 1, 1)[:, 0:1]
    same = qcol == qrow[0:1, :]
    before = iota((count, count), 0) < iota((count, count), 1)
    after = iota((count, count), 1) < iota((count, count), 0)
    rank_row = jnp.sum(jnp.where(same & before, 1.0, 0.0), axis=0, keepdims=True)
    rank_col = jnp.sum(jnp.where(same & after, 1.0, 0.0), axis=1, keepdims=True)
    my_section = mine[0:1, 0:1].astype(F32)
    slot = (iota((SLOTS, count), 0) % READERS).astype(F32)
    pick = jnp.where((qrow[0:1, :] == my_section) & (rank_row == slot), 1.0, 0.0).astype(BF16)
    picked = dot(pick, sq_ref[...]).astype(BF16)
    low_rows = iota((SLOTS, HD), 0) < READERS
    qx = jnp.where(low_rows, picked[:, 0:HD].astype(F32), picked[:, HD:].astype(F32)).astype(BF16)
    q_flat = jnp.concatenate([q_ref[:, 0:HD], q_ref[:, HD : 2 * HD]], axis=0)

    def relay(k):
        gather_copy(k).wait_recv()
        relay_copy(k).start()

    each(1, chips, relay)
    others = sec.at[pl.ds(0, n - 1)]
    pltpu.make_async_copy(others, others, sc_recv).wait()
    each(0, chips, lambda k: relay_copy(k).wait_recv())

    sections = sec[...].reshape(n, HD).astype(F32).astype(BF16)

    block_spans = min(CHUNK // rows, n)
    width = block_spans * rows

    def scores_of(at):
        blocks = kv[pl.ds(at * block_spans, block_spans)].reshape(width, 2 * HD)
        keys = blocks[:, 0:HD]
        vals = blocks[:, HD : 2 * HD]
        s = dot(q_flat, keys, 1, 1) * scale
        x = dot(qx, keys, 1, 1) * scale
        spread = (
            iota((n, width), 0) == (iota((n, width), 1) // rows + at * block_spans)
        ).astype(BF16)
        token_section = dot(sections[:, 0:SLOTS], spread, 0, 0)
        mask = token_section == my_section
        return s, x, mask, vals

    def one(at, state):
        s, x, mask, vals = scores_of(at)
        top0, total0, acc0, xtop0, xtotal0 = state
        top = jnp.maximum(top0, jnp.max(s, axis=1, keepdims=True))
        shrink = jnp.exp(top0 - top)
        w = jnp.exp(s - top)
        total = total0 * shrink + jnp.sum(w, axis=1, keepdims=True)
        acc = acc0 * shrink + dot(w.astype(BF16), vals)
        xtop = jnp.maximum(
            xtop0, jnp.max(jnp.where(mask, x, F32(-1e30)), axis=1, keepdims=True)
        )
        xw = jnp.where(mask, jnp.exp(x - xtop), F32(0.0))
        xtotal = xtotal0 * jnp.exp(xtop0 - xtop) + jnp.sum(xw, axis=1, keepdims=True)
        return top, total, acc, xtop, xtotal

    state = (
        jnp.full((rows * HQ, 1), -1e30, F32),
        jnp.zeros((rows * HQ, 1), F32),
        jnp.zeros((rows * HQ, HD), F32),
        jnp.full((SLOTS, 1), -1e30, F32),
        jnp.zeros((SLOTS, 1), F32),
    )
    if n // block_spans == 1:
        state = one(0, state)
    else:
        state = lax.fori_loop(0, n // block_spans, one, state)
    top, total, acc, xtop, xtotal = state
    ctx = (acc / total).astype(BF16)
    own_x = dot(qx, kv[me][:, 0:HD], 1, 1) * scale
    own_w = jnp.exp(own_x - xtop).astype(BF16)
    p0 = dot(own_w, ctx[0:rows])
    p1 = dot(own_w, ctx[rows : 2 * rows])
    part[...] = (jnp.where(low_rows, p0, p1) / xtotal).astype(BF16)

    def part_copy(k):
        return remote(part, gath.at[me], pt_send, pt_recv, lax.rem(me + k, n))

    each(1, n, lambda k: part_copy(k).start())
    gath[me] = part[...]
    ctx_ref[:, 0:HD] = ctx[0:rows]
    ctx_ref[:, HD : 2 * HD] = ctx[rows : 2 * rows]

    wide = n * SLOTS
    tall = HQ * count
    owner = (iota((n, wide), 0) == iota((n, wide), 1) // SLOTS).astype(BF16)
    slot_section = dot(sections[:, 0:8], owner, 0, 0)[0:1, :]
    slot_rank = (iota((1, wide), 1) % READERS).astype(F32)
    slot_head = (iota((1, wide), 1) % SLOTS) // READERS
    hits = (qcol == slot_section) & (rank_col == slot_rank)
    choose = jnp.concatenate(
        [jnp.where(hits & (slot_head == h), 1.0, 0.0) for h in range(HQ)], axis=0
    ).astype(BF16)

    for w in weights:
        w.wait()
    seen = gath.at[pl.ds(0, n - 1)]
    pltpu.make_async_copy(seen, seen, pt_recv).wait()
    rows_in = gath[...].astype(F32).reshape(wide, HD).astype(BF16)
    pooled = dot(choose, rows_in).astype(BF16)
    pooled = jnp.concatenate([pooled[0:count], pooled[count:tall]], axis=1)
    embed = dot(pooled, ov[...])
    inv = lax.rsqrt(jnp.mean(embed * embed, axis=1, keepdims=True) + 1e-06)
    normed = (embed * inv * gain_ref[...].astype(F32)).astype(BF16)
    hidden = jax.nn.gelu(dot(normed, upv[...]), approximate=True).astype(BF16)

    span = out_ref.shape[1]
    y = dot(hidden, downv[...])
    for d in range(n):
        yb[d % 2, d // 2] = y[:, d * span : (d + 1) * span].astype(BF16)
    pair = remote(yb.at[1 - core], rb, pr_send, pr_recv, partner)
    pair.start()
    pair.wait_recv()

    def final_copy(k):
        to = lax.rem(chip + k, chips)
        return remote(
            sb.at[to], fb.at[k - 1], fn_send.at[k - 1], fn_recv.at[k - 1], to * 2 + core
        )

    def join(k):
        to = lax.rem(chip + k, chips)
        sb[to] = (yb[core, to].astype(F32) + rb[to].astype(F32)).astype(BF16)
        final_copy(k).start()

    each(1, chips, join)
    result = yb[core, chip].astype(F32) + rb[chip].astype(F32)
    if chips <= 16:
        for k in range(1, chips):
            final_copy(k).wait_recv()
            result = result + fb[k - 1].astype(F32)
    else:

        def take(k, value):
            final_copy(k).wait_recv()
            return value + fb[k - 1].astype(F32)

        result = lax.fori_loop(1, chips, take, result)
    out_ref[...] = result.astype(BF16)

    each(1, chips, lambda k: gather_copy(k).wait_send())
    each(0, chips, lambda k: relay_copy(k).wait_send())
    pltpu.make_async_copy(others, others, sc_send).wait()
    pltpu.make_async_copy(seen, seen, pt_send).wait()
    pair.wait_send()
    each(1, chips, lambda k: final_copy(k).wait_send())


def per_device(
    n,
    queries,
    keys,
    values,
    span_section,
    query_section,
    section_queries,
    out_proj,
    norm_gain,
    up_weight,
    down_weight,
):
    rows = queries.shape[0]
    count = section_queries.shape[0]
    features = out_proj.shape[1]
    span = features // n
    chips = n // 2
    dma = pltpu.SemaphoreType.DMA
    vmem = pl.BlockSpec(memory_space=pltpu.VMEM)
    smem = pl.BlockSpec(memory_space=pltpu.SMEM)
    anyw = pl.BlockSpec(memory_space=pl.ANY)
    return pl.pallas_call(
        functools.partial(kernel, n),
        out_shape=(
            jax.ShapeDtypeStruct(queries.shape, BF16),
            jax.ShapeDtypeStruct((count, span), BF16),
        ),
        in_specs=[vmem, anyw, anyw, smem, vmem, vmem, anyw, vmem, anyw, anyw],
        out_specs=(vmem, vmem),
        scratch_shapes=[
            pltpu.VMEM((n, rows, 2 * HD), BF16),
            pltpu.VMEM((n, 1, HD), jnp.int32),
            pltpu.VMEM((SLOTS, HD), BF16),
            pltpu.VMEM((n, SLOTS, HD), BF16),
            pltpu.VMEM(out_proj.shape, BF16),
            pltpu.VMEM(up_weight.shape, BF16),
            pltpu.VMEM(down_weight.shape, BF16),
            pltpu.VMEM((2, chips, count, span), BF16),
            pltpu.VMEM((chips, count, span), BF16),
            pltpu.VMEM((chips, count, span), BF16),
            pltpu.VMEM((chips - 1, count, span), BF16),
            dma((3,)),
            dma((2,)),
            dma((chips - 1,)),
            dma((chips - 1,)),
            dma((chips,)),
            dma((chips,)),
            dma,
            dma,
            dma,
            dma,
            dma,
            dma,
            dma((chips - 1,)),
            dma((chips - 1,)),
        ],
        compiler_params=pltpu.CompilerParams(
            collective_id=0, has_side_effects=True, vmem_limit_bytes=60 * 1024 * 1024
        ),
    )(
        queries,
        keys,
        values,
        span_section.reshape(1, 1),
        query_section.reshape(1, count),
        section_queries,
        out_proj,
        norm_gain.reshape(1, features),
        up_weight,
        down_weight,
    )


def solution(mesh):
    n = mesh.shape["ctx"]
    in_specs = (
        P(("groups", "ctx"), None),
        P(("groups", "ctx"), None),
        P(("groups", "ctx"), None),
        P(("groups", "ctx")),
        P("groups"),
        P("groups", None),
        P(),
        P(),
        P(None, "ctx"),
        P("ctx", None),
    )
    out_specs = (P(("groups", "ctx"), None), P("groups", "ctx"))
    return jax.shard_map(
        functools.partial(per_device, n),
        mesh=mesh,
        in_specs=in_specs,
        out_specs=out_specs,
        check_vma=False,
    )
```

```python
import functools

import jax
import jax.numpy as jnp
from jax import lax
from jax.experimental import pallas as pl
from jax.experimental.pallas import tpu as pltpu
from jax.sharding import PartitionSpec as P

HD = 128
HQ = 2
SPAN = 64
READERS = 4
MARK = 8
CHUNK = 1024
SLOTS = HQ * READERS

F32 = jnp.float32
BF16 = jnp.bfloat16
MESH = pl.DeviceIdType.MESH


def each(low, high, body):
    if high - low <= 16:
        for k in range(low, high):
            body(k)
    else:
        pl.loop(low, high)(body)


def dims(a, b):
    return (((a,), (b,)), ((), ()))


def dot(a, b, ca=1, cb=0):
    return lax.dot_general(a, b, dims(ca, cb), preferred_element_type=F32)


def iota(shape, axis):
    return lax.broadcasted_iota(jnp.int32, shape, axis)


def kernel(
    n,
    q_ref,
    k_ref,
    v_ref,
    span_ref,
    qsec_ref,
    sq_ref,
    o_ref,
    gain_ref,
    up_ref,
    down_ref,
    ctx_ref,
    out_ref,
    qv,
    qsecv,
    sqv,
    gainv,
    ctxv,
    outv,
    kv,
    part,
    gath,
    ov,
    upv,
    downv,
    yb,
    rb,
    sb,
    fb,
    wsem,
    kvsem,
    z_send,
    z_recv,
    y_send,
    y_recv,
    c_send,
    c_recv,
    pt_send,
    pt_recv,
    pr_send,
    pr_recv,
    fn_send,
    fn_recv,
):
    scale = HD ** (-0.5)
    chips = n // 2
    line = n // 4
    me = lax.axis_index("ctx")
    chip = me // 2
    core = me % 2
    row = me // 4
    side = chip % 2
    partner = me + 1 - 2 * core
    across = me + 2 - 4 * side
    rows = q_ref.shape[0]
    tokens = n * rows
    count = qsec_ref.shape[1]

    own = kv.at[me]
    kcopy = pltpu.make_async_copy(k_ref, own.at[0:rows, 0:HD], kvsem.at[0])
    vcopy = pltpu.make_async_copy(v_ref, own.at[0:rows, HD : 2 * HD], kvsem.at[1])
    small = [
        pltpu.make_async_copy(src, dst, wsem.at[3 + i])
        for i, (src, dst) in enumerate(
            ((qsec_ref, qsecv), (sq_ref, sqv), (q_ref, qv), (gain_ref, gainv))
        )
    ]
    weights = [
        pltpu.make_async_copy(o_ref, ov, wsem.at[0]),
        pltpu.make_async_copy(up_ref, upv, wsem.at[1]),
        pltpu.make_async_copy(down_ref, downv, wsem.at[2]),
    ]
    kcopy.start()
    vcopy.start()

    barrier = pltpu.get_barrier_semaphore()

    def greet(to):
        pl.semaphore_signal(barrier, inc=1, device_id={"ctx": to}, device_id_type=MESH)

    greet(partner)
    greet(across)

    @pl.when(row > 0)
    def _():
        greet(me - 4)

    @pl.when(row < line - 1)
    def _():
        greet(me + 4)

    for c in small + weights:
        c.start()
    mine = jnp.broadcast_to(span_ref[0, 0], (1, HD))
    kv[me, rows : rows + MARK] = jnp.broadcast_to(span_ref[0, 0], (MARK, 2 * HD)).astype(
        F32
    ).astype(BF16)
    kcopy.wait()
    vcopy.wait()
    pl.semaphore_wait(barrier, 2 + jnp.minimum(row, 1) + jnp.minimum(line - 1 - row, 1))

    def remote(src, dst, send, recv, to):
        return pltpu.make_async_remote_copy(
            src_ref=src,
            dst_ref=dst,
            send_sem=send,
            recv_sem=recv,
            device_id={"ctx": to},
            device_id_type=MESH,
        )

    def line_copy(at, send, to):
        block = kv.at[at * 4 + side * 2 + core]
        return remote(block, block, z_send.at[send], z_recv.at[at], to)

    def cross_copy(at, there):
        block = kv.at[at * 4 + there * 2 + core]
        return remote(block, block, y_send.at[at], y_recv.at[at], across)

    def pair_copy(at, there, mate):
        block = kv.at[at * 4 + there * 2 + mate]
        sem = there * line + at
        return remote(block, block, c_send.at[sem], c_recv.at[sem], partner)

    def spread_row(at):
        cross_copy(at, side).start()
        pair_copy(at, side, core).start()

    @pl.when(row < line - 1)
    def _():
        line_copy(row, row, me + 4).start()

    @pl.when(row > 0)
    def _():
        line_copy(row, line, me - 4).start()

    spread_row(row)

    for c in small:
        c.wait()
    qrow = jnp.broadcast_to(qsecv[...], (8, count)).astype(F32)
    eye = (iota((count, count), 0) == iota((count, count), 1)).astype(BF16)
    qcol = dot(eye, qrow.astype(BF16), 1, 1)[:, 0:1]
    same = qcol == qrow[0:1, :]
    before = iota((count, count), 0) < iota((count, count), 1)
    after = iota((count, count), 1) < iota((count, count), 0)
    rank_row = jnp.sum(jnp.where(same & before, 1.0, 0.0), axis=0, keepdims=True)
    rank_col = jnp.sum(jnp.where(same & after, 1.0, 0.0), axis=1, keepdims=True)
    my_section = mine[0:1, 0:1].astype(F32)
    slot = (iota((SLOTS, count), 0) % READERS).astype(F32)
    pick = jnp.where((qrow[0:1, :] == my_section) & (rank_row == slot), 1.0, 0.0).astype(BF16)
    picked = dot(pick, sqv[...]).astype(BF16)
    low_rows = iota((SLOTS, HD), 0) < READERS
    qx = jnp.where(low_rows, picked[:, 0:HD].astype(F32), picked[:, HD:].astype(F32)).astype(BF16)
    q_flat = jnp.concatenate([qv[:, 0:HD], qv[:, HD : 2 * HD]], axis=0)

    def from_across(at):
        cross_copy(at, 1 - side).wait_recv()
        pair_copy(at, 1 - side, core).start()

    def relay(k):
        @pl.when(row >= k)
        def _():
            line_copy(row - k, row - k, partner).wait_recv()

            @pl.when(row < line - 1)
            def _():
                line_copy(row - k, row - k, me + 4).start()

            spread_row(row - k)

        @pl.when(row + k < line)
        def _():
            line_copy(row + k, row + k, partner).wait_recv()

            @pl.when(row > 0)
            def _():
                line_copy(row + k, row + k, me - 4).start()

            spread_row(row + k)

        behind(k - 1)

    def behind(k):
        @pl.when(row >= k)
        def _():
            from_across(row - k)

        if not isinstance(k, int) or k > 0:

            @pl.when((row + k < line) & (k > 0))
            def _():
                from_across(row + k)

    each(1, line, relay)
    behind(line - 1)
    each(0, line, lambda k: pair_copy(k, 0, 1 - core).wait_recv())
    each(0, line, lambda k: pair_copy(k, 1, 1 - core).wait_recv())

    sections = kv[:, rows : rows + MARK, 0:HD].astype(F32)[:, 0, :].astype(BF16)

    block_spans = min(CHUNK // rows, n)
    width = block_spans * rows

    def scores_of(at):
        span_at = pl.ds(at * block_spans, block_spans)
        keys = kv[span_at, 0:rows, 0:HD].reshape(width, HD)
        vals = kv[span_at, 0:rows, HD : 2 * HD].reshape(width, HD)
        s = dot(q_flat, keys, 1, 1) * scale
        x = dot(qx, keys, 1, 1) * scale
        spread = (
            iota((n, width), 0) == (iota((n, width), 1) // rows + at * block_spans)
        ).astype(BF16)
        token_section = dot(sections[:, 0:SLOTS], spread, 0, 0)
        mask = token_section == my_section
        return s, x, mask, vals

    def one(at, state):
        s, x, mask, vals = scores_of(at)
        top0, total0, acc0, xtop0, xtotal0 = state
        top = jnp.maximum(top0, jnp.max(s, axis=1, keepdims=True))
        shrink = jnp.exp(top0 - top)
        w = jnp.exp(s - top)
        total = total0 * shrink + jnp.sum(w, axis=1, keepdims=True)
        acc = acc0 * shrink + dot(w.astype(BF16), vals)
        xtop = jnp.maximum(
            xtop0, jnp.max(jnp.where(mask, x, F32(-1e30)), axis=1, keepdims=True)
        )
        xw = jnp.where(mask, jnp.exp(x - xtop), F32(0.0))
        xtotal = xtotal0 * jnp.exp(xtop0 - xtop) + jnp.sum(xw, axis=1, keepdims=True)
        return top, total, acc, xtop, xtotal

    state = (
        jnp.full((rows * HQ, 1), -1e30, F32),
        jnp.zeros((rows * HQ, 1), F32),
        jnp.zeros((rows * HQ, HD), F32),
        jnp.full((SLOTS, 1), -1e30, F32),
        jnp.zeros((SLOTS, 1), F32),
    )
    if n // block_spans == 1:
        state = one(0, state)
    else:
        state = lax.fori_loop(0, n // block_spans, one, state)
    top, total, acc, xtop, xtotal = state
    ctx = (acc / total).astype(BF16)
    own_x = dot(qx, kv[me, 0:rows, 0:HD], 1, 1) * scale
    own_w = jnp.exp(own_x - xtop).astype(BF16)
    p0 = dot(own_w, ctx[0:rows])
    p1 = dot(own_w, ctx[rows : 2 * rows])
    part[...] = (jnp.where(low_rows, p0, p1) / xtotal).astype(BF16)

    def part_copy(k):
        return remote(part, gath.at[me], pt_send, pt_recv, lax.rem(me + k, n))

    each(1, n, lambda k: part_copy(k).start())
    gath[me] = part[...]
    ctxv[:, 0:HD] = ctx[0:rows]
    ctxv[:, HD : 2 * HD] = ctx[rows : 2 * rows]
    ctx_out = pltpu.make_async_copy(ctxv, ctx_ref, kvsem.at[0])
    ctx_out.start()
    gain = gainv[...].astype(F32)
    gain = jnp.concatenate([gain[i : i + 1] for i in range(gain.shape[0])], axis=1)

    wide = n * SLOTS
    tall = HQ * count
    owner = (iota((n, wide), 0) == iota((n, wide), 1) // SLOTS).astype(BF16)
    slot_section = dot(sections[:, 0:8], owner, 0, 0)[0:1, :]
    slot_rank = (iota((1, wide), 1) % READERS).astype(F32)
    slot_head = (iota((1, wide), 1) % SLOTS) // READERS
    hits = (qcol == slot_section) & (rank_col == slot_rank)
    choose = jnp.concatenate(
        [jnp.where(hits & (slot_head == h), 1.0, 0.0) for h in range(HQ)], axis=0
    ).astype(BF16)

    for w in weights:
        w.wait()
    seen = gath.at[pl.ds(0, n - 1)]
    pltpu.make_async_copy(seen, seen, pt_recv).wait()
    rows_in = gath[...].astype(F32).reshape(wide, HD).astype(BF16)
    pooled = dot(choose, rows_in).astype(BF16)
    pooled = jnp.concatenate([pooled[0:count], pooled[count:tall]], axis=1)
    embed = dot(pooled, ov[...])
    inv = lax.rsqrt(jnp.mean(embed * embed, axis=1, keepdims=True) + 1e-06)
    normed = (embed * inv * gain).astype(BF16)
    hidden = jax.nn.gelu(dot(normed, upv[...]), approximate=True).astype(BF16)

    span = out_ref.shape[1]
    y = dot(hidden, downv[...])
    for d in range(n):
        yb[d % 2, d // 2] = y[:, d * span : (d + 1) * span].astype(BF16)
    pair = remote(yb.at[1 - core], rb, pr_send, pr_recv, partner)
    pair.start()
    pair.wait_recv()

    def final_copy(k):
        to = lax.rem(chip + k, chips)
        return remote(
            sb.at[to], fb.at[k - 1], fn_send.at[k - 1], fn_recv.at[k - 1], to * 2 + core
        )

    def join(k):
        to = lax.rem(chip + k, chips)
        sb[to] = (yb[core, to].astype(F32) + rb[to].astype(F32)).astype(BF16)
        final_copy(k).start()

    each(1, chips, join)
    result = yb[core, chip].astype(F32) + rb[chip].astype(F32)
    if chips <= 16:
        for k in range(1, chips):
            final_copy(k).wait_recv()
            result = result + fb[k - 1].astype(F32)
    else:

        def take(k, value):
            final_copy(k).wait_recv()
            return value + fb[k - 1].astype(F32)

        result = lax.fori_loop(1, chips, take, result)
    outv[...] = result.astype(BF16)
    final_out = pltpu.make_async_copy(outv, out_ref, kvsem.at[1])
    final_out.start()

    @pl.when(row < line - 1)
    def _():
        line_copy(row, row, partner).wait_send()

    @pl.when(row > 0)
    def _():
        line_copy(row, line, partner).wait_send()

    def sent(at):
        @pl.when(((at < row) & (row < line - 1)) | ((at > row) & (row > 0)))
        def _():
            line_copy(at, at, partner).wait_send()

        cross_copy(at, side).wait_send()
        pair_copy(at, 0, core).wait_send()
        pair_copy(at, 1, core).wait_send()

    each(0, line, sent)
    pltpu.make_async_copy(seen, seen, pt_send).wait()
    pair.wait_send()
    each(1, chips, lambda k: final_copy(k).wait_send())
    ctx_out.wait()
    final_out.wait()


def hand_over(a_ref, b_ref, c_ref, d_ref, av, bv, sems):
    into = (
        pltpu.make_async_copy(a_ref, av, sems.at[0]),
        pltpu.make_async_copy(b_ref, bv, sems.at[1]),
    )
    out = (
        pltpu.make_async_copy(av, c_ref, sems.at[2]),
        pltpu.make_async_copy(bv, d_ref, sems.at[3]),
    )
    for c in into:
        c.start()
    for c, o in zip(into, out):
        c.wait()
        o.start()
    for o in out:
        o.wait()


def per_device(
    n,
    queries,
    keys,
    values,
    span_section,
    query_section,
    section_queries,
    out_proj,
    norm_gain,
    up_weight,
    down_weight,
):
    rows = queries.shape[0]
    count = section_queries.shape[0]
    features = out_proj.shape[1]
    span = features // n
    chips = n // 2
    line = n // 4
    dma = pltpu.SemaphoreType.DMA
    vmem = pl.BlockSpec(memory_space=pltpu.VMEM)
    smem = pl.BlockSpec(memory_space=pltpu.SMEM)
    anyw = pl.BlockSpec(memory_space=pl.ANY)
    result = pl.pallas_call(
        functools.partial(kernel, n),
        out_shape=(
            jax.ShapeDtypeStruct(queries.shape, BF16),
            jax.ShapeDtypeStruct((count, span), BF16),
        ),
        in_specs=[anyw, anyw, anyw, smem, anyw, anyw, anyw, anyw, anyw, anyw],
        out_specs=(anyw, anyw),
        scratch_shapes=[
            pltpu.VMEM(queries.shape, BF16),
            pltpu.VMEM((1, count), jnp.int32),
            pltpu.VMEM(section_queries.shape, BF16),
            pltpu.VMEM((features // HD, HD), BF16),
            pltpu.VMEM(queries.shape, BF16),
            pltpu.VMEM((count, span), BF16),
            pltpu.VMEM((n, rows + MARK, 2 * HD), BF16),
            pltpu.VMEM((SLOTS, HD), BF16),
            pltpu.VMEM((n, SLOTS, HD), BF16),
            pltpu.VMEM(out_proj.shape, BF16),
            pltpu.VMEM(up_weight.shape, BF16),
            pltpu.VMEM(down_weight.shape, BF16),
            pltpu.VMEM((2, chips, count, span), BF16),
            pltpu.VMEM((chips, count, span), BF16),
            pltpu.VMEM((chips, count, span), BF16),
            pltpu.VMEM((chips - 1, count, span), BF16),
            dma((7,)),
            dma((2,)),
            dma((line + 1,)),
            dma((line,)),
            dma((line,)),
            dma((line,)),
            dma((chips,)),
            dma((chips,)),
            dma,
            dma,
            dma,
            dma,
            dma((chips - 1,)),
            dma((chips - 1,)),
        ],
        compiler_params=pltpu.CompilerParams(
            collective_id=0, has_side_effects=True, vmem_limit_bytes=60 * 1024 * 1024
        ),
    )(
        queries,
        keys,
        values,
        span_section.reshape(1, 1),
        query_section.reshape(1, count),
        section_queries,
        out_proj,
        norm_gain.reshape(features // HD, HD),
        up_weight,
        down_weight,
    )
    return pl.pallas_call(
        hand_over,
        out_shape=(
            jax.ShapeDtypeStruct(queries.shape, BF16),
            jax.ShapeDtypeStruct((count, span), BF16),
        ),
        in_specs=[anyw, anyw],
        out_specs=(anyw, anyw),
        scratch_shapes=[
            pltpu.VMEM(queries.shape, BF16),
            pltpu.VMEM((count, span), BF16),
            dma((4,)),
        ],
    )(*result)


def solution(mesh):
    n = mesh.shape["ctx"]
    in_specs = (
        P(("groups", "ctx"), None),
        P(("groups", "ctx"), None),
        P(("groups", "ctx"), None),
        P(("groups", "ctx")),
        P("groups"),
        P("groups", None),
        P(),
        P(),
        P(None, "ctx"),
        P("ctx", None),
    )
    out_specs = (P(("groups", "ctx"), None), P("groups", "ctx"))
    return jax.shard_map(
        functools.partial(per_device, n),
        mesh=mesh,
        in_specs=in_specs,
        out_specs=out_specs,
        check_vma=False,
    )
```
